256 devices in a mesh: gx: 4 (over y), gy: 8 (over z), gz: 8 (over x, core).
Axes of the slice: x: 4, y: 4, z: 8, core: 2. Of those that a mesh axis runs over, the one named last changes fastest.
Arguments:
- populations: float32 [19, 16, 128, 1024], P(None, 'gx', 'gy', 'gz'), may hold values from 0.02 to 0.12
- solid: int32 [16, 128, 1024], P('gx', 'gy', 'gz'), may hold values 0 or 1
- coefficients: float32 [2048, 16, 256], P(('gx', 'gz')), may hold values from -0.09375 to 0.09375
- body_nodes: float32 [3, 512, 2048], P(None, 'gy', ('gx', 'gz')), may hold values from -2 to 2
- centers: float32 [3, 2048], P(None, ('gx', 'gz')), may hold values from -0.5 to 0.5
- angles: float32 [3, 2048], P(None, ('gx', 'gz')), may hold values from -3.140625 to 3.140625
- velocity: float32 [6, 2048], P(None, ('gx', 'gz')), may hold values from -0.5 to 0.5
- node_frac: float32 [3, 512, 2048], P(None, 'gy', ('gx', 'gz')), may hold values from 0 to 1
- node_cell: int32 [512, 2048], P('gy', ('gx', 'gz')), may hold values from 0 to 6014, as said below
- grain_tile: int32 [8, 2048, 1], P('gy', ('gx', 'gz')), may hold values from 0 to 31; in each aligned block of 64 rows (0 to 63, 64 to 127, ..., all dimensions but the last counted through in order) at most 4 rows name the same one
- send_grain: int32 [32, 128], P(('gx', 'gz')), may hold values from -1 to 63, as said below
- recv_partner: int32 [32, 128], P(('gx', 'gz')), may hold values from -1 to 63, as said below
Outputs:
- populations_out: float32 [19, 16, 128, 1024], P(None, 'gx', 'gy', 'gz')
- centers_out: float32 [3, 2048], P(None, ('gx', 'gz'))
- velocity_out: float32 [6, 2048], P(None, ('gx', 'gz'))
The draws below stay inside these ranges and needn't reach their ends.
Inputs may be any that keep to these rules, and one draw needn't show every extreme that they name: `node_cell`: c = (x * 16 + y) * 128 + z with x < 3, y < 15, z < 127, so all eight corners lie in the tile. `grain_tile`: in the rows of one device at most 4 grains name the same tile, a bound that some block reaches. `send_grain`: -1 marks an empty slot; within each destination's 4 slots the live ones come first; slot k for destination d on source s is live exactly when slot k for source s on owner d is live in recv_partner; some owner receives all 4 slots live from every source. `recv_partner`: -1 marks an empty slot, matching send_grain as stated there.
All inputs are finite; a program needn't handle non-finite values. No bound on the sum of `solid` on one device may be relied on, other than what follows from the above.
Results may differ from the reference program's by a relative error of at most 0.0001.
Values sent between devices are 32-bit elements; how exact they have to be, the bound alone decides.
No kernel may reach another device: no remote copies, remote signals or barrier semaphores. Data moves between devices by JAX's collectives and lax.ppermute only.
A program may use at most 128 MiB of HBM per device.

```python
import math
import jax
import jax.numpy as jnp
import numpy as np
from jax import lax

Q = 19
ORDER = 16
NODES = 512
STEPS = 2
GR_OWN = 64
CX = 4
CY = 16
CZ = 128
CAP = 4
OWNERS = 32
TILES_Z = 8
GRAINS = 2048
SLAB = 64
TILE_CAP = 4
NX = 16
NY = 128
NZ = 1024
N_GY = 8


def contact_live(key):
    base_key = jax.random.fold_in(key, 11)
    first_key, second_key, third_key = jax.random.split(base_key, 3)
    lowest = max(1, CAP // 4)
    levels = jax.random.randint(first_key, (OWNERS,), lowest, CAP + 1)
    busiest = jax.random.randint(second_key, (), 0, OWNERS)
    is_busiest = jnp.arange(OWNERS) == busiest
    levels = jnp.where(is_busiest, CAP, levels)
    spread = levels - levels // 2 + 1
    counts = jax.random.randint(third_key, (OWNERS, OWNERS), 0, 1 << 20) % spread[None, :] + (levels // 2)[None, :]
    counts = jnp.where(is_busiest[None, :], CAP, counts)
    slots = jnp.arange(CAP)
    return slots[None, None, :] < counts[:, :, None]


def draw_send_grain(key, part):
    live = contact_live(key)
    picks = jax.random.randint(jax.random.fold_in(key, 12), (OWNERS, OWNERS, CAP), 0, GR_OWN)
    return jnp.where(live, picks, -1).reshape(OWNERS, OWNERS * CAP).astype(jnp.int32)


def draw_recv_partner(key, part):
    live = jnp.transpose(contact_live(key), (1, 0, 2))
    picks = jax.random.randint(jax.random.fold_in(key, 13), (OWNERS, OWNERS, CAP), 0, GR_OWN)
    return jnp.where(live, picks, -1).reshape(OWNERS, OWNERS * CAP).astype(jnp.int32)


def draw_node_cell(key, part):
    key_x, key_y, key_z = jax.random.split(jax.random.fold_in(key, 14), 3)
    along_x = jax.random.randint(key_x, (NODES, GRAINS), 0, CX - 1)
    along_y = jax.random.randint(key_y, (NODES, GRAINS), 0, CY - 1)
    along_z = jax.random.randint(key_z, (NODES, GRAINS), 0, CZ - 1)
    return ((along_x * CY + along_y) * CZ + along_z).astype(jnp.int32)


def touch_ends(entries, own_key, low, high):
    extent = entries.shape
    index_at = [jax.random.randint(jax.random.fold_in(own_key, axis), (), 0, extent[axis]) for axis in range(len(extent))]
    entries = entries.at[tuple(index_at)].set(low)
    longest = extent.index(max(extent))
    index_at[longest] = (index_at[longest] + 1) % extent[longest]
    return entries.at[tuple(index_at)].set(high)


def shard_levels(own_key, extent, cuts, smallest, largest):
    factor_of, own = 1.0, jax.random.fold_in(own_key, 6)
    for position, parts in cuts:
        steps = jnp.exp(jax.random.uniform(jax.random.fold_in(own, position), (parts,), jnp.float32, smallest / len(cuts), largest / len(cuts)))
        factor_of = factor_of * jnp.repeat(steps, extent[position] // parts).reshape([-1 if axis == position else 1 for axis in range(len(extent))])
    return factor_of


def deal_out(rng, own, number, rows, amount, top, most, skew):
    order = jax.random.permutation(rng, amount)
    packed, usual = shares(amount, rows * top, most, skew, True), shares(amount, rows * top, most, skew, False)
    places = jnp.arange(amount)

    def named(lengths, offset_by):
        used = int((lengths > 0).sum())
        fixed = max(1, used // 4)
        moved = fixed + (places - fixed + offset_by * (used - fixed)) % max(1, amount - fixed)
        return jnp.zeros((amount,), jnp.int32).at[order[jnp.where(places < fixed, places, moved)]].set(jnp.asarray(lengths, jnp.int32))

    lengths = jnp.where(number % 4 == 0, named(packed, number // 4), named(usual, number - number // 4 - 1))
    mixed = jax.random.permutation(jax.random.fold_in(own, 3), amount)
    giver, taker = mixed[0:amount // 2 * 2:2], mixed[1:amount // 2 * 2:2]
    margin = jnp.minimum(lengths[giver] - 1, most - lengths[taker]) // 2
    margin = jnp.where((giver == order[0]) | (taker == order[0]) | (lengths[taker] == 0), 0, jnp.maximum(margin, 0))
    moved = jax.random.randint(jax.random.fold_in(own, 4), (amount // 2,), 0, 1 << 20) % (margin + 1)
    lengths = lengths.at[giver].add(-moved).at[taker].add(moved)
    items = jnp.searchsorted(jnp.cumsum(lengths), jnp.arange(rows * top), side="right").astype(jnp.int32)
    listing = items.reshape(top, rows).T
    listing = listing[jax.random.permutation(jax.random.fold_in(own, 1), rows)]
    offset_by = jax.random.randint(jax.random.fold_in(own, 2), (rows, 1), 0, top)
    return jnp.take_along_axis(listing, (jnp.arange(top)[None, :] + offset_by) % top, axis=1)


def shares(number_of, total, bound, skew, full):
    portions = [(1 << 20) // math.isqrt(grade ** skew) + 1 for grade in range(1, number_of + 1)]
    largest = bound if full else min(bound, max(-(-total // number_of), total * portions[0] // sum(portions)))
    least = 1 if total - largest >= number_of - 1 else 0
    holding, rest = [largest] + [least] * (number_of - 1), total - largest - least * (number_of - 1)
    while rest > 0:
        candidates = [i for i in range(1, number_of) if holding[i] < largest] or [i for i in range(1, number_of) if holding[i] < bound]
        pool, remaining = sum([portions[i] for i in candidates]), rest
        for i in candidates:
            extra = min(bound - holding[i], max(1, remaining * portions[i] // pool), rest)
            holding[i] = holding[i] + extra
            rest = rest - extra
    return np.array(holding)


def noise(rng, shape, width, limit, shards=(), kind=jnp.bfloat16):
    values = width * jax.random.normal(rng, shape, jnp.float32)
    if shards:
        values = values * shard_levels(rng, shape, shards, -0.22, 0.18)
    return jnp.clip(values, -limit, limit).astype(kind)


def setup_inputs(seed: int = 0) -> dict:
    streams_of = jax.random.split(jax.random.key(seed), 13)
    populations = jnp.clip(0.02 + 0.09999999776482582 * jax.random.uniform(streams_of[0], (Q, NX, NY, NZ), jnp.float32) ** shard_levels(streams_of[0], (Q, NX, NY, NZ), ((1, 4), (2, 8), (3, 8)), -0.2, 0.2), 0.02, 0.12)
    solid = touch_ends((jax.random.randint(streams_of[1], (NX, NY, NZ), 0, 6) < 1).astype(jnp.int32), jax.random.fold_in(streams_of[1], 1), 0, 1)
    coefficients = noise(streams_of[2], (GRAINS, ORDER, ORDER * ORDER), (1.0 / (4 * ORDER)), 0.09375, ((0, 32),), jnp.float32)
    body_nodes = noise(streams_of[3], (3, NODES, GRAINS), 0.4, 2.0, ((1, 8), (2, 32)), jnp.float32)
    centers = jnp.clip(jax.random.uniform(streams_of[4], (3, GRAINS), jnp.float32, -0.5, 0.5) * shard_levels(streams_of[4], (3, GRAINS), ((1, 32),), -0.4, 0.0), -0.5, 0.5)
    angles = jnp.clip(jax.random.uniform(streams_of[5], (3, GRAINS), jnp.float32, -3.140625, 3.140625), -3.140625, 3.140625)
    velocity = noise(streams_of[6], (6, GRAINS), 0.1, 0.5, ((1, 32),), jnp.float32)
    node_frac = jnp.clip(1.0 * jax.random.uniform(streams_of[7], (3, NODES, GRAINS), jnp.float32) ** shard_levels(streams_of[7], (3, NODES, GRAINS), ((1, 8), (2, 32)), -0.2, 0.2), 0.0, 1.0)
    node_cell = draw_node_cell(jax.random.fold_in(streams_of[12], 71), 0)
    grain_tile_keys = jax.random.split(jax.random.fold_in(streams_of[9], 1), N_GY * GRAINS // GR_OWN)
    grain_tile_turns = jax.random.permutation(jax.random.fold_in(streams_of[9], 3), N_GY * GRAINS // GR_OWN)
    grain_tile = jax.vmap(lambda own, number: deal_out(jax.random.fold_in(streams_of[9], 2), own, number, GR_OWN, OWNERS, 1, TILE_CAP, 2))(grain_tile_keys, grain_tile_turns).reshape((N_GY, GRAINS, 1))
    send_grain = draw_send_grain(jax.random.fold_in(streams_of[12], 71), 0)
    recv_partner = draw_recv_partner(jax.random.fold_in(streams_of[12], 71), 0)
    return dict(populations=populations, solid=solid, coefficients=coefficients, body_nodes=body_nodes, centers=centers, angles=angles, velocity=velocity, node_frac=node_frac, node_cell=node_cell, grain_tile=grain_tile, send_grain=send_grain, recv_partner=recv_partner)


highest = lax.Precision.HIGHEST
lattice_dirs = np.array([[0, 0, 0], [1, 0, 0], [-1, 0, 0], [0, 1, 0], [0, -1, 0], [0, 0, 1], [0, 0, -1], [1, 1, 0], [-1, -1, 0], [1, -1, 0], [-1, 1, 0], [1, 0, 1], [-1, 0, -1], [1, 0, -1], [-1, 0, 1], [0, 1, 1], [0, -1, -1], [0, 1, -1], [0, -1, 1]], dtype=np.int32)
lattice_float = lattice_dirs.astype(np.float32)
lattice_weights = np.array([1.0 / 3.0] + [1.0 / 18.0] * 6 + [1.0 / 36.0] * 12, dtype=np.float32)
opposite_dirs = np.array([0, 2, 1, 4, 3, 6, 5, 8, 7, 10, 9, 12, 11, 14, 13, 16, 15, 18, 17], dtype=np.int32)
tau_relax = 0.9
ib_stiffness = 0.5
contact_stiffness = 0.05
time_step = 0.05

def compose(left, right):
    return jnp.einsum('ijg,jkg->ikg', left, right, precision=highest)

def cross_product(left, right):
    return jnp.stack([left[1] * right[2] - left[2] * right[1], left[2] * right[0] - left[0] * right[2], left[0] * right[1] - left[1] * right[0]])

def rotation_from(angles):
    cosine_a, sine_a = (jnp.cos(angles[0]), jnp.sin(angles[0]))
    cosine_b, sine_b = (jnp.cos(angles[1]), jnp.sin(angles[1]))
    cosine_c, sine_c = (jnp.cos(angles[2]), jnp.sin(angles[2]))
    unit = jnp.ones_like(cosine_a)
    empty = jnp.zeros_like(cosine_a)
    about_x = jnp.stack([jnp.stack([unit, empty, empty]), jnp.stack([empty, cosine_a, -sine_a]), jnp.stack([empty, sine_a, cosine_a])])
    about_y = jnp.stack([jnp.stack([cosine_b, empty, sine_b]), jnp.stack([empty, unit, empty]), jnp.stack([-sine_b, empty, cosine_b])])
    about_z = jnp.stack([jnp.stack([cosine_c, -sine_c, empty]), jnp.stack([sine_c, cosine_c, empty]), jnp.stack([empty, empty, unit])])
    return compose(about_z, compose(about_y, about_x))

def chebyshev(coords, order):
    first_kind = [jnp.ones_like(coords), coords]
    second_kind = [jnp.ones_like(coords), 2.0 * coords]
    for degree in range(2, order):
        first_kind.append(2.0 * coords * first_kind[-1] - first_kind[-2])
        second_kind.append(2.0 * coords * second_kind[-1] - second_kind[-2])
    slopes = [jnp.zeros_like(coords)] + [degree * second_kind[degree - 1] for degree in range(1, order)]
    return (jnp.stack(first_kind[:order]), jnp.stack(slopes))

def contact_forces(coefs, rotation, centre, nodes):
    order = coefs.shape[1]
    count = nodes.shape[1]
    pieces = coefs.shape[0]
    relative = nodes - centre[:, None, :]
    local = jnp.clip(jnp.einsum('jib,jnb->inb', rotation, relative, precision=highest), -1.0, 1.0)
    poly_x, slope_x = chebyshev(local[0], order)
    poly_y, slope_y = chebyshev(local[1], order)
    poly_z, slope_z = chebyshev(local[2], order)
    along_z = jnp.concatenate([poly_z, slope_z], axis=1)
    table = coefs.reshape(pieces, order * order, order)
    partial_sum = jnp.einsum('brc,cmb->rmb', table, along_z, precision=highest).reshape(order, order, 2 * count, pieces)
    value_part = jnp.einsum('abnk,bnk->ank', partial_sum[:, :, :count], poly_y, precision=highest)
    slope_zpart = jnp.einsum('abnk,bnk->ank', partial_sum[:, :, count:], poly_y, precision=highest)
    slope_ypart = jnp.einsum('abnk,bnk->ank', partial_sum[:, :, :count], slope_y, precision=highest)
    level = lax.optimization_barrier(jnp.sum(value_part * poly_x, axis=0))
    gradient = jnp.stack([lax.optimization_barrier(jnp.sum(value_part * slope_x, axis=0)), lax.optimization_barrier(jnp.sum(slope_ypart * poly_x, axis=0)), lax.optimization_barrier(jnp.sum(slope_zpart * poly_x, axis=0))])
    depth = jnp.maximum(-level, 0.0)
    strength = contact_stiffness * depth / jnp.sqrt(1.0 + lax.optimization_barrier(jnp.sum(gradient * gradient, axis=0)))
    return jnp.einsum('ijb,jnb->inb', rotation, gradient, precision=highest) * strength[None]

def moments(flat):
    density = lax.optimization_barrier(jnp.sum(flat, axis=0))
    momentum = jnp.einsum('qa,qc->ac', lattice_float, flat, precision=highest)
    return (density, momentum / density[None])

def collide(flat, density, fluid_velocity, force, solid_flat):
    shifted = fluid_velocity + tau_relax * force / density[None]
    along = jnp.einsum('qa,ac->qc', lattice_float, shifted, precision=highest)
    speed = lax.optimization_barrier(jnp.sum(shifted * shifted, axis=0))
    balance = lattice_weights[:, None] * density[None] * (1.0 + 3.0 * along + 4.5 * along * along - 1.5 * speed[None])
    relaxed = flat - (flat - balance) / tau_relax
    return jnp.where(solid_flat[None] > 0, flat, relaxed)

def corner_terms(frac, base, stride_x, stride_y):
    terms = []
    for offset_x in (0, 1):
        weight_x = frac[0] if offset_x else 1.0 - frac[0]
        for offset_y in (0, 1):
            weight_y = frac[1] if offset_y else 1.0 - frac[1]
            for offset_z in (0, 1):
                weight_z = frac[2] if offset_z else 1.0 - frac[2]
                terms.append((base + offset_x * stride_x + offset_y * stride_y + offset_z, weight_x * weight_y * weight_z))
    return terms

def advance(centre, motion, rotation, totals):
    motion = motion + time_step * totals
    centre = centre + time_step * motion[0:3]
    spin = motion[3:6]
    empty = jnp.zeros_like(spin[0])
    skew = jnp.stack([jnp.stack([empty, -spin[2], spin[1]]), jnp.stack([spin[2], empty, -spin[0]]), jnp.stack([-spin[1], spin[0], empty])])
    rotation = rotation + time_step * compose(skew, rotation)
    return (centre, motion, rotation)

def reference(populations, solid, coefficients, body_nodes, centers, angles, velocity, node_frac, node_cell, grain_tile, send_grain, recv_partner):
    owners = OWNERS
    grains = GRAINS
    sends = jnp.transpose(send_grain.reshape(owners, owners, CAP), (1, 0, 2))
    recvs = recv_partner.reshape(owners, owners, CAP)
    source = jnp.broadcast_to(jnp.arange(owners, dtype=jnp.int32)[None, :, None], recvs.shape)
    target = jnp.broadcast_to(jnp.arange(owners, dtype=jnp.int32)[:, None, None], recvs.shape)
    alive_all = (recvs >= 0).reshape(-1).astype(jnp.float32)
    partner = (source * GR_OWN + jnp.maximum(sends, 0)).reshape(-1).astype(jnp.int32)
    holder = (target * GR_OWN + jnp.maximum(recvs, 0)).reshape(-1).astype(jnp.int32)
    pairs = owners * owners * CAP
    block = math.gcd(pairs, 8)
    dest_node = jnp.repeat(grain_tile[:, :, 0], SLAB, axis=0)
    tile_x = dest_node // TILES_Z
    tile_z = dest_node % TILES_Z
    tile_y = (jnp.arange(NODES, dtype=jnp.int32) // SLAB)[:, None]
    local_x = node_cell // (CY * CZ)
    local_y = node_cell // CZ % CY
    local_z = node_cell % CZ
    base = ((tile_x * CX + local_x) * NY + tile_y * CY + local_y) * NZ + tile_z * CZ + local_z
    corners = corner_terms(node_frac, base, NY * NZ, NZ)
    solid_flat = solid.reshape(-1)
    rotation = rotation_from(angles)
    centre = centers
    motion = velocity
    fluid = populations
    for step in range(STEPS):
        arm = jnp.einsum('ijg,jng->ing', rotation, body_nodes, precision=highest)
        positions = centre[:, None, :] + arm
        node_speed = motion[0:3, None, :] + cross_product(motion[3:6, None, :], arm)

        def pair_block(start):
            hold = lax.dynamic_slice_in_dim(holder, start, block)
            part = lax.dynamic_slice_in_dim(partner, start, block)
            alive = lax.dynamic_slice_in_dim(alive_all, start, block)
            nodes = positions[:, :, part]
            forces = contact_forces(coefficients[hold], rotation[:, :, hold], centre[:, hold], nodes) * alive[None, None, :]
            on_holder = jnp.concatenate([-lax.optimization_barrier(jnp.sum(forces, axis=1)), lax.optimization_barrier(jnp.sum(cross_product(nodes - centre[:, hold][:, None, :], -forces), axis=1))])
            on_partner = jnp.concatenate([lax.optimization_barrier(jnp.sum(forces, axis=1)), lax.optimization_barrier(jnp.sum(cross_product(nodes - centre[:, part][:, None, :], forces), axis=1))])
            return (on_holder, on_partner)
        holder_terms, partner_terms = lax.map(pair_block, jnp.arange(0, pairs, block, dtype=jnp.int32))
        holder_terms = jnp.moveaxis(holder_terms, 1, 0).reshape(6, pairs)
        partner_terms = jnp.moveaxis(partner_terms, 1, 0).reshape(6, pairs)
        loads = jax.ops.segment_sum(holder_terms.T, holder, num_segments=grains).T + jax.ops.segment_sum(partner_terms.T, partner, num_segments=grains).T
        flat = fluid.reshape(Q, NX * NY * NZ)
        density, fluid_velocity = moments(flat)
        interp = jnp.zeros(node_speed.shape, jnp.float32)
        for index, weight in corners:
            interp = interp + weight[None] * fluid_velocity[:, index]
        node_force = ib_stiffness * (node_speed - interp)
        cell_force = jnp.zeros((3, NX * NY * NZ), jnp.float32)
        for index, weight in corners:
            cell_force = cell_force.at[:, index].add(weight[None] * node_force)
        totals = loads + jnp.concatenate([-lax.optimization_barrier(jnp.sum(node_force, axis=1)), lax.optimization_barrier(jnp.sum(cross_product(arm, -node_force), axis=1))])
        post = collide(flat, density, fluid_velocity, cell_force, solid_flat).reshape(Q, NX, NY, NZ)
        moved = jnp.stack([jnp.roll(post[direction], shift=tuple((int(value) for value in lattice_dirs[direction])), axis=(0, 1, 2)) for direction in range(Q)])
        fluid = jnp.where(solid[None] > 0, moved[opposite_dirs], moved)
        centre, motion, rotation = advance(centre, motion, rotation, totals)
    return (fluid, centre, motion)
```

```python
import functools

import jax
import jax.numpy as jnp
import numpy as np
from jax import lax
from jax.experimental import pallas as pl
from jax.experimental.pallas import tpu as pltpu
from jax.sharding import PartitionSpec as P

F32, BF16, I32 = jnp.float32, jnp.bfloat16, jnp.int32

DIRS = [
    (0, 0, 0),
    (1, 0, 0),
    (-1, 0, 0),
    (0, 1, 0),
    (0, -1, 0),
    (0, 0, 1),
    (0, 0, -1),
    (1, 1, 0),
    (-1, -1, 0),
    (1, -1, 0),
    (-1, 1, 0),
    (1, 0, 1),
    (-1, 0, -1),
    (1, 0, -1),
    (-1, 0, 1),
    (0, 1, 1),
    (0, -1, -1),
    (0, 1, -1),
    (0, -1, 1),
]
WEIGHTS = [float(np.float32(1.0 / 3.0))] + [float(np.float32(1.0 / 18.0))] * 6
WEIGHTS = WEIGHTS + [float(np.float32(1.0 / 36.0))] * 12
OPPOSITE = [0, 2, 1, 4, 3, 6, 5, 8, 7, 10, 9, 12, 11, 14, 13, 16, 15, 18, 17]
TAU = 0.9
STIFF = 0.5
CONTACT = 0.05
DT = 0.05
PLUS = [[q for q in range(19) if DIRS[q][axis] == 1] for axis in range(3)]
MINUS = [[q for q in range(19) if DIRS[q][axis] == -1] for axis in range(3)]


def iota(shape, dim):
    return lax.broadcasted_iota(I32, shape, dim)


def split2(x):
    high = x.astype(BF16)
    return high, (x - high.astype(F32)).astype(BF16)


def split3(x):
    high = x.astype(BF16)
    rest = x - high.astype(F32)
    middle = rest.astype(BF16)
    return high, middle, (rest - middle.astype(F32)).astype(BF16)


def dot(a, b):
    return lax.dot_general(a, b, (((1,), (0,)), ((), ())), preferred_element_type=F32)


def dot_nt(a, b):
    return lax.dot_general(a, b, (((1,), (1,)), ((), ())), preferred_element_type=F32)


def lanes_half():
    return iota((64, 128), 1) < 64


def slot_lane_ids():
    p = iota((64, 128), 0)
    return (p & 31) * 4 + (p >> 5) * 2 + (iota((64, 128), 1) >> 6)


def slot_onehot(row):
    p = iota((64, 128), 0)
    first = (p & 31) * 4 + (p >> 5) * 2
    lane = iota((64, 128), 1)
    col_a = jnp.sum(jnp.where(lane == first, row, 0.0), axis=1, keepdims=True)
    col_b = jnp.sum(jnp.where(lane == first + 1, row, 0.0), axis=1, keepdims=True)
    named = jnp.where(lanes_half(), col_a, col_b)
    return jnp.where(named == (lane & 63).astype(F32), 1.0, 0.0)


def tile_onehot(route2, route_col):
    lane = iota((64, 128), 1)
    same = (route2 == route_col) & (iota((64, 128), 0) < (lane & 63))
    rank = jnp.sum(jnp.where(same, 1.0, 0.0), axis=0, keepdims=True)
    slot = route2 * 4.0 + rank
    return jnp.where(slot == slot_lane_ids().astype(F32), 1.0, 0.0)


def field(state, f):
    return jnp.where(lanes_half(), state[:, f : f + 1], state[:, 64 + f : 65 + f])


def strided(ref, count, stride, first):
    return jnp.concatenate(
        [ref[pl.ds(first + h, count, stride=stride), :] for h in range(2)], axis=0
    )


def store_strided(ref, value, stride, first):
    for h in range(2):
        ref[pl.ds(first + h, 32, stride=stride), :] = value[h * 32 : (h + 1) * 32]


def cross(a, b):
    return [
        a[1] * b[2] - a[2] * b[1],
        a[2] * b[0] - a[0] * b[2],
        a[0] * b[1] - a[1] * b[0],
    ]


def lane_sums(values, firsts):
    lane = iota((64, 128), 1)
    half = lanes_half()
    out = jnp.zeros((64, 128), F32)
    for value, first in zip(values, firsts):
        sum_a = jnp.sum(jnp.where(half, value, 0.0), axis=1, keepdims=True)
        sum_b = jnp.sum(jnp.where(half, 0.0, value), axis=1, keepdims=True)
        out = jnp.where(lane == first, sum_a, out)
        out = jnp.where(lane == 64 + first, sum_b, out)
    return out


def pack_kernel(
    body, frac, cell, centers, angles, velocity, send, route2, route_col, out, state, spread
):
    ca, sa = jnp.cos(angles[0:1, :]), jnp.sin(angles[0:1, :])
    cb, sb = jnp.cos(angles[1:2, :]), jnp.sin(angles[1:2, :])
    cc, sc = jnp.cos(angles[2:3, :]), jnp.sin(angles[2:3, :])
    rows = [
        cc * cb,
        cc * sb * sa - sc * ca,
        cc * sb * ca + sc * sa,
        sc * cb,
        sc * sb * sa + cc * ca,
        sc * sb * ca - cc * sa,
        -sb,
        cb * sa,
        cb * ca,
    ]
    state[...] = jnp.zeros((24, 64), F32)
    for i, row in enumerate(rows):
        state[i : i + 1, :] = row
    state[9:12, :] = centers[...]
    state[12:18, :] = velocity[...]
    spread[...] = jnp.zeros((1024, 128), F32)
    for c in range(8):
        if c < 3:
            value = body[c]
        elif c < 6:
            value = frac[c - 3]
        elif c == 6:
            value = (cell[...] + 1).astype(F32)
        else:
            value = state[...]
        count = value.shape[0]
        for h in range(2):
            first = c * 128 + h * 64
            spread[first : first + count, h * 64 : h * 64 + 64] = value
    tile_hot = tile_onehot(route2[...], route_col[...]).astype(BF16)
    pair_hot = slot_onehot(send[...]).astype(BF16)
    for c in range(8):
        parts = split3(spread[c * 128 : (c + 1) * 128, :])
        picked = dot_nt(tile_hot, parts[2]) + dot_nt(tile_hot, parts[1])
        store_strided(out, picked + dot_nt(tile_hot, parts[0]), 24, 2 * c)
        if c < 3 or c == 7:
            picked = dot_nt(pair_hot, parts[2]) + dot_nt(pair_hot, parts[1])
            picked = picked + dot_nt(pair_hot, parts[0])
            store_strided(out, picked, 24, 16 + 2 * min(c, 3))


def table_kernel(coefs, out):
    parts = split3(coefs[...].reshape(1024, 256))
    source = iota((256, 256), 0)
    lane = iota((256, 256), 1)
    within = lane & 127
    ranges = ((0, 48), (48, 80), (80, 96))
    for b in range(0, 16, 2):
        wanted = (b + (lane >> 7)) * 16 + (within & 15)
        total = None
        for part, (low, high) in zip(parts, ranges):
            pick = (source == wanted) & (within >= low) & (within < high)
            term = dot(part, jnp.where(pick, 1.0, 0.0).astype(BF16))
            total = term if total is None else total + term
        total = total.astype(BF16)
        for k in range(2):
            piece = total[:, k * 128 : (k + 1) * 128].reshape(64, 16, 128)
            out[:, (b + k) * 16 : (b + k + 1) * 16, :] = piece


def contact_kernel(
    own_first,
    partner_first,
    partner_stride,
    partners,
    bodies,
    partner_state,
    state,
    recv_row,
    hydro,
    table,
    payload,
    local,
    zt,
    zs,
    yt,
    ys,
    xt,
    xs,
    found,
):
    pst = strided(partner_state, 32, partner_stride, partner_first)
    body = [strided(bodies, 32, 24, 16 + 2 * c) for c in range(3)]
    hold_hot = slot_onehot(recv_row[...])
    own = jnp.concatenate([state[...], jnp.zeros((40, 64), F32)], axis=0)
    parts = split3(own)
    hot_a = hold_hot[:, :64].astype(BF16)
    hot_b = hold_hot[:, 64:].astype(BF16)
    own_a = dot_nt(hot_a, parts[2]) + dot_nt(hot_a, parts[1]) + dot_nt(hot_a, parts[0])
    own_b = dot_nt(hot_b, parts[2]) + dot_nt(hot_b, parts[1]) + dot_nt(hot_b, parts[0])
    half = lanes_half()

    def held(f):
        return jnp.where(half, own_a[:, f : f + 1], own_b[:, f : f + 1])

    arm = []
    for i in range(3):
        arm.append(
            field(pst, 3 * i) * body[0]
            + field(pst, 3 * i + 1) * body[1]
            + field(pst, 3 * i + 2) * body[2]
        )
    rel = [arm[i] + (field(pst, 9 + i) - held(9 + i)) for i in range(3)]
    rot = [[held(3 * i + j) for j in range(3)] for i in range(3)]
    for axis, (kinds, slopes) in enumerate(((xt, xs), (yt, ys), (zt, zs))):
        y = rot[0][axis] * rel[0] + rot[1][axis] * rel[1] + rot[2][axis] * rel[2]
        y = jnp.clip(y, -1.0, 1.0)
        twice = 2.0 * y
        t_old, t_new = jnp.ones((64, 128), F32), y
        u_old, u_new = jnp.zeros((64, 128), F32), jnp.ones((64, 128), F32)
        kinds[pl.ds(0, 64, stride=16), :] = t_old
        slopes[pl.ds(0, 64, stride=16), :] = u_old
        for n in range(1, 16):
            kinds[pl.ds(n, 64, stride=16), :] = t_new
            slopes[pl.ds(n, 64, stride=16), :] = float(n) * u_new
            t_old, t_new = t_new, twice * t_new - t_old
            u_old, u_new = u_new, twice * u_new - u_old
    low = iota((16, 128), 1) < 64
    zero = jnp.zeros((16, 256), BF16)

    def one(p):
        slot = (p & 31) * 4 + (p >> 5) * 2
        grain_a = jnp.maximum(partners[0, slot], 0)
        grain_b = jnp.maximum(partners[0, slot + 1], 0)
        left = jnp.concatenate([table[grain_a], table[grain_b]], axis=1)
        at = pl.ds(pl.multiple_of(p * 16, 16), 16)
        z_value, z_slope = zt[at, :], zs[at, :]
        blocks = []
        for keep in (low, jnp.logical_not(low)):
            value = split3(jnp.where(keep, z_value, 0.0))
            slope = split3(jnp.where(keep, z_slope, 0.0))
            both = [jnp.concatenate([value[i], slope[i]], axis=1) for i in range(3)]
            blocks += [both[0], both[1], both[2], both[0], both[1], both[0], zero, zero]
        right = jnp.concatenate(blocks, axis=0)
        sums = dot(left, right)
        y_kind, y_slope = yt[at, :], ys[at, :]
        value = jnp.zeros((16, 128), F32)
        value_y = jnp.zeros((16, 128), F32)
        value_z = jnp.zeros((16, 128), F32)
        for b in range(16):
            plain = sums[b * 16 : (b + 1) * 16, :128]
            steep = sums[b * 16 : (b + 1) * 16, 128:]
            value = value + plain * y_kind[b : b + 1]
            value_y = value_y + plain * y_slope[b : b + 1]
            value_z = value_z + steep * y_kind[b : b + 1]
        x_kind, x_slope = xt[at, :], xs[at, :]
        for i, term in enumerate(
            (value * x_kind, value * x_slope, value_y * x_kind, value_z * x_kind)
        ):
            found[i, pl.ds(p, 1), :] = jnp.sum(term, axis=0, keepdims=True)

    def two(i, carry):
        one(2 * i)
        one(2 * i + 1)
        return carry

    lax.fori_loop(0, 32, two, 0)
    level = found[0]
    grad = [found[1], found[2], found[3]]
    alive = jnp.sum(hold_hot.reshape(64, 128) * jnp.where(half, 1.0, 0.0), axis=1, keepdims=True)
    alive_b = jnp.sum(hold_hot * jnp.where(half, 0.0, 1.0), axis=1, keepdims=True)
    alive = jnp.where(half, alive, alive_b)
    norm = 1.0 + grad[0] * grad[0] + grad[1] * grad[1] + grad[2] * grad[2]
    strength = alive * (CONTACT * jnp.maximum(-level, 0.0) / jnp.sqrt(norm))
    force = [
        (rot[i][0] * grad[0] + rot[i][1] * grad[1] + rot[i][2] * grad[2]) * strength
        for i in range(3)
    ]
    on_holder = cross(rel, force)
    on_partner = cross(arm, force)
    summed = lane_sums(force + on_partner + on_holder, [0, 1, 2, 3, 4, 5, 18, 19, 20])
    lane = iota((64, 128), 1) & 63
    store_strided(payload, jnp.where(lane < 6, summed, hydro[...]), 2, 0)
    local[...] = summed


def node_setup(recv, refs):
    fx, fy, fz, base, alive = refs
    fx[...] = strided(recv, 32, 24, 6)
    fy[...] = strided(recv, 32, 24, 8)
    fz[...] = strided(recv, 32, 24, 10)
    named = strided(recv, 32, 24, 12)
    base[...] = jnp.maximum(named.astype(I32) - 1, 0)
    alive[...] = jnp.where(named > 0.5, 1.0, 0.0)


def node_weights(refs, p):
    fx, fy, fz, base, _ = refs
    at = pl.ds(p, 1)
    cell = base[at, :]
    x, y, z = cell >> 11, (cell >> 7) & 15, cell & 127
    gap = iota((128, 128), 0) - z
    up = fz[at, :]
    along_z = jnp.where(gap == 0, 1.0 - up, jnp.where(gap == 1, up, 0.0))
    gap = iota((16, 128), 0) - y
    up = fy[at, :]
    along_y = jnp.where(gap == 0, 1.0 - up, jnp.where(gap == 1, up, 0.0))
    up = fx[at, :]
    both = []
    for cx in range(4):
        weight = jnp.where(x == cx, 1.0 - up, jnp.where(x == cx - 1, up, 0.0))
        both.append(weight * along_y)
    return split2(along_z), jnp.concatenate(both, axis=0)


def pair_weights(refs, i):
    first, second = node_weights(refs, 2 * i), node_weights(refs, 2 * i + 1)
    high = jnp.concatenate([first[0][0], second[0][0]], axis=1)
    low = jnp.concatenate([first[0][1], second[0][1]], axis=1)
    return high, low, jnp.concatenate([first[1], second[1]], axis=1)


def moments(get):
    density = None
    flow = [None, None, None]
    for q in range(19):
        value = get(q)
        density = value if density is None else density + value
        for axis in range(3):
            if DIRS[q][axis] == 0:
                continue
            if flow[axis] is None:
                flow[axis] = value if DIRS[q][axis] > 0 else -value
            elif DIRS[q][axis] > 0:
                flow[axis] = flow[axis] + value
            else:
                flow[axis] = flow[axis] - value
    return density, [f / density for f in flow]


def flow_operand(flow, operand):
    for axis in range(3):
        high, low = split2(flow[axis])
        rows = slice(axis * 64, axis * 64 + 64)
        operand[rows, 0:128] = high
        operand[rows, 128:256] = high
        operand[rows, 256:384] = low


def interpolate(operand, high, low, across):
    along = dot(operand[...], jnp.concatenate([high, low, high], axis=0))
    return [
        jnp.sum(along[c * 64 : (c + 1) * 64] * across, axis=0, keepdims=True) for c in range(3)
    ]


def spread_pair(total, force, high, low, across):
    push = jnp.concatenate([force[c] * across for c in range(3)], axis=0)
    push_high, push_low = split2(push)
    total[...] += dot_nt(
        jnp.concatenate([push_high, push_low], axis=0), jnp.concatenate([high, low], axis=0)
    )


def node_speed(recv, state):
    body = [strided(recv, 32, 24, 2 * c) for c in range(3)]
    arm = [
        field(state, 3 * i) * body[0]
        + field(state, 3 * i + 1) * body[1]
        + field(state, 3 * i + 2) * body[2]
        for i in range(3)
    ]
    spin = [field(state, 15 + i) for i in range(3)]
    turned = cross(spin, arm)
    return [field(state, 12 + i) + turned[i] for i in range(3)]


def hydro_sums(recv, interp):
    body = [strided(recv, 32, 24, 2 * c) for c in range(3)]
    values = [interp[c] for c in range(3)]
    values += [body[j] * interp[k] for j in range(3) for k in range(3)]
    return lane_sums(values, list(range(6, 18)))


def collide(get, density, flow, total, solid, post, y_up, y_down):
    wall = solid[...].reshape(64, 128) > 0
    scale = TAU / density
    moved = []
    for c in range(3):
        rows = slice(c * 64, (c + 1) * 64)
        lows = slice(192 + c * 64, 192 + (c + 1) * 64)
        push = total[rows, 0:128] + (total[rows, 128:256] + total[lows, 0:128])
        moved.append(flow[c] + scale * push)
    speed = moved[0] * moved[0] + moved[1] * moved[1] + moved[2] * moved[2]
    base = 1.0 - 1.5 * speed
    for q in range(19):
        along = None
        for axis in range(3):
            if DIRS[q][axis] == 0:
                continue
            term = moved[axis] if DIRS[q][axis] > 0 else -moved[axis]
            along = term if along is None else along + term
        bracket = base if along is None else base + along * (3.0 + 4.5 * along)
        value = get(q)
        relaxed = value - (value - WEIGHTS[q] * density * bracket) * (1.0 / TAU)
        post[q] = jnp.where(wall, value, relaxed)
    for i in range(5):
        for x in range(4):
            row = i * 4 + x
            y_up[row : row + 1, :] = post[PLUS[1][i], x * 16 + 15 : x * 16 + 16, :]
            y_down[row : row + 1, :] = post[MINUS[1][i], x * 16 : x * 16 + 1, :]


def first_fluid_kernel(
    recv, fluid, solid, post, y_up, y_down, hydro, operand, total, interp, speeds, *refs
):
    get = lambda q: fluid[q].reshape(64, 128)
    density, flow = moments(get)
    flow_operand(flow, operand)
    node_setup(recv, refs)
    speed = node_speed(recv, strided(recv, 32, 24, 14))
    for c in range(3):
        speeds[c] = speed[c]
    total[...] = jnp.zeros((384, 256), F32)
    alive = refs[4]

    def pair(i, carry):
        high, low, across = pair_weights(refs, i)
        found = interpolate(operand, high, low, across)
        force = []
        for c in range(3):
            sides = []
            for k in range(2):
                at = pl.ds(2 * i + k, 1)
                side = found[c][:, k * 128 : (k + 1) * 128]
                interp[c, at, :] = side
                sides.append(STIFF * (speeds[c, at, :] - side) * alive[at, :])
            force.append(jnp.concatenate(sides, axis=1))
        spread_pair(total, force, high, low, across)
        return carry

    lax.fori_loop(0, 32, pair, 0)
    hydro[...] = hydro_sums(recv, interp)
    collide(get, density, flow, total, solid, post, y_up, y_down)


def shifted_y(post, q, x, y_low, y_high):
    value = post[q, x * 16 : (x + 1) * 16, :]
    step = DIRS[q][1]
    if step == 0:
        return value
    row = iota((16, 128), 0)
    if step > 0:
        at = PLUS[1].index(q) * 4 + x
        return jnp.where(row == 0, y_low[at : at + 1, :], pltpu.roll(value, 1, 0))
    at = MINUS[1].index(q) * 4 + x
    return jnp.where(row == 15, y_high[at : at + 1, :], pltpu.roll(value, 15, 0))


def shifted_yx(post, q, x, y_low, y_high, x_low, x_high):
    source = x - DIRS[q][0]
    if source < 0:
        at = PLUS[0].index(q) * 16
        return x_low[at : at + 16, :]
    if source > 3:
        at = MINUS[0].index(q) * 16
        return x_high[at : at + 16, :]
    return shifted_y(post, q, source, y_low, y_high)


def faces_x_kernel(post, y_low, y_high, x_up, x_down):
    for i in range(5):
        rows = slice(i * 16, (i + 1) * 16)
        x_up[rows, :] = shifted_y(post, PLUS[0][i], 3, y_low, y_high)
        x_down[rows, :] = shifted_y(post, MINUS[0][i], 0, y_low, y_high)


def faces_z_kernel(post, y_low, y_high, x_low, x_high, z_up, z_down):
    lane = iota((16, 128), 1)
    up = jnp.zeros((16, 128), F32)
    down = jnp.zeros((16, 128), F32)
    for i in range(5):
        for x in range(4):
            value = shifted_yx(post, PLUS[2][i], x, y_low, y_high, x_low, x_high)
            up = jnp.where(lane == i * 4 + x, value[:, 127:128], up)
            value = shifted_yx(post, MINUS[2][i], x, y_low, y_high, x_low, x_high)
            down = jnp.where(lane == i * 4 + x, value[:, 0:1], down)
    z_up[...] = up
    z_down[...] = down


def stream(post, solid, halos, out):
    y_low, y_high, x_low, x_high, z_low, z_high = halos
    lane = iota((16, 128), 1)

    def moved(q, x):
        value = shifted_yx(post, q, x, y_low, y_high, x_low, x_high)
        step = DIRS[q][2]
        if step == 0:
            return value
        if step > 0:
            at = PLUS[2].index(q) * 4 + x
            return jnp.where(lane == 0, z_low[:, at : at + 1], pltpu.roll(value, 1, 1))
        at = MINUS[2].index(q) * 4 + x
        return jnp.where(lane == 127, z_high[:, at : at + 1], pltpu.roll(value, 127, 1))

    for x in range(4):
        wall = solid[x] > 0
        for q in range(19):
            other = OPPOSITE[q]
            if other < q:
                continue
            value = moved(q, x)
            if other == q:
                out[q, x] = value
                continue
            back = moved(other, x)
            out[q, x] = jnp.where(wall, back, value)
            out[other, x] = jnp.where(wall, value, back)


def stream_kernel(post, solid, *refs):
    stream(post, solid, refs[:6], refs[6])


def stream_interp_kernel(post, solid, recv, *refs):
    halos = refs[:6]
    fluid, hydro, interp, operand = refs[6:10]
    scratch = refs[10:]
    stream(post, solid, halos, fluid)
    _, flow = moments(lambda q: fluid[q].reshape(64, 128))
    flow_operand(flow, operand)
    node_setup(recv, scratch)

    def pair(i, carry):
        high, low, across = pair_weights(scratch, i)
        found = interpolate(operand, high, low, across)
        for c in range(3):
            for k in range(2):
                at = pl.ds(2 * i + k, 1)
                interp[c, at, :] = found[c][:, k * 128 : (k + 1) * 128]
        return carry

    lax.fori_loop(0, 32, pair, 0)
    hydro[...] = hydro_sums(recv, interp)


def second_fluid_kernel(
    recv, states, fluid, solid, interp, post, y_up, y_down, total, speeds, *refs
):
    get = lambda q: fluid[q].reshape(64, 128)
    density, flow = moments(get)
    node_setup(recv, refs)
    alive = refs[4]
    speed = node_speed(recv, strided(states, 32, 4, 2))
    for c in range(3):
        speeds[c] = STIFF * (speed[c] - interp[c]) * alive[...]
    total[...] = jnp.zeros((384, 256), F32)

    def pair(i, carry):
        high, low, across = pair_weights(refs, i)
        force = [
            jnp.concatenate([speeds[c, pl.ds(2 * i + k, 1), :] for k in range(2)], axis=1)
            for c in range(3)
        ]
        spread_pair(total, force, high, low, across)
        return carry

    lax.fori_loop(0, 32, pair, 0)
    collide(get, density, flow, total, solid, post, y_up, y_down)


def by_grain(value, hot):
    turned = jnp.transpose(jnp.concatenate([value, jnp.zeros((64, 128), F32)], axis=0))
    out = None
    for h in range(2):
        for part in split3(turned[h * 64 : (h + 1) * 64, 0:64]):
            term = dot(part, hot[:, h * 64 : (h + 1) * 64].astype(BF16))
            out = term if out is None else out + term
    return out


def rotation_rows(state):
    return [[state[3 * i + j : 3 * i + j + 1, :] for j in range(3)] for i in range(3)]


def matmul3(a, b):
    return [
        [a[i][0] * b[0][k] + a[i][1] * b[1][k] + a[i][2] * b[2][k] for k in range(3)]
        for i in range(3)
    ]


def spin_matrix(w):
    zero = jnp.zeros_like(w[0])
    return [[zero, -w[2], w[1]], [w[2], zero, -w[0]], [-w[1], w[0], zero]]


def loads_kernel(back, local, state, body, send, recv_row, route2, route_col, out):
    returned = strided(back, 32, 2, 0)
    on_partner = by_grain(returned, slot_onehot(send[...]))
    fluid_sums = by_grain(returned, tile_onehot(route2[...], route_col[...]))
    on_holder = by_grain(local[...], slot_onehot(recv_row[...]))
    state = state[...]
    rot = rotation_rows(state)
    velocity = [state[12 + i : 13 + i, :] for i in range(3)]
    spin = [state[15 + i : 16 + i, :] for i in range(3)]
    turn = matmul3(spin_matrix(spin), rot)
    nodes = [body[c] for c in range(3)]
    first = [jnp.sum(nodes[c], axis=0, keepdims=True) for c in range(3)]
    pairs = [[None] * 3 for _ in range(3)]
    for i in range(3):
        for j in range(i, 3):
            pairs[i][j] = jnp.sum(nodes[i] * nodes[j], axis=0, keepdims=True)
            pairs[j][i] = pairs[i][j]
    interp = [fluid_sums[6 + c : 7 + c, :] for c in range(3)]
    mixed = [[fluid_sums[9 + 3 * j + k : 10 + 3 * j + k, :] for k in range(3)] for j in range(3)]
    count = float(body.shape[1])
    transposed = [[turn[j][i] for j in range(3)] for i in range(3)]
    arm = [rot[i][0] * first[0] + rot[i][1] * first[1] + rot[i][2] * first[2] for i in range(3)]
    carried = [turn[i][0] * first[0] + turn[i][1] * first[1] + turn[i][2] * first[2] for i in range(3)]
    outer = matmul3(rot, matmul3(pairs, transposed))
    drag = matmul3(rot, mixed)
    lever = cross(arm, velocity)
    out8 = []
    for i in range(3):
        force = count * velocity[i] + carried[i] - interp[i]
        total = on_partner[i : i + 1] - on_holder[i : i + 1] - STIFF * force
        out8.append(total)
    for i in range(3):
        j, k = (i + 1) % 3, (i + 2) % 3
        force = lever[i] + (outer[j][k] - outer[k][j]) - (drag[j][k] - drag[k][j])
        total = on_partner[3 + i : 4 + i] - on_holder[18 + i : 19 + i] - STIFF * force
        out8.append(total)
    for row, value in enumerate(out8):
        for copy in range(8):
            out[copy * 8 + row : copy * 8 + row + 1, 0:64] = value


def advance(totals, state):
    total = totals[0:8, 0:64]
    for copy in range(1, 8):
        total = total + totals[copy * 8 : copy * 8 + 8, 0:64]
    state = state[...]
    motion = [state[12 + i : 13 + i, :] + DT * total[i : i + 1, :] for i in range(6)]
    centre = [state[9 + i : 10 + i, :] + DT * motion[i] for i in range(3)]
    rot = rotation_rows(state)
    change = matmul3(spin_matrix(motion[3:6]), rot)
    rows = [rot[i][j] + DT * change[i][j] for i in range(3) for j in range(3)]
    return rows + centre + motion


def middle_kernel(totals, state, send, route2, route_col, out, fresh, spread):
    fresh[...] = jnp.zeros((24, 64), F32)
    for i, row in enumerate(advance(totals, state)):
        fresh[i : i + 1, :] = row
    spread[...] = jnp.zeros((128, 128), F32)
    spread[0:24, 0:64] = fresh[...]
    spread[64:88, 64:128] = fresh[...]
    parts = split3(spread[...])
    hots = (slot_onehot(send[...]), tile_onehot(route2[...], route_col[...]))
    for at, hot in enumerate(hots):
        hot = hot.astype(BF16)
        picked = dot_nt(hot, parts[2]) + dot_nt(hot, parts[1]) + dot_nt(hot, parts[0])
        store_strided(out, picked, 4, 2 * at)


def last_kernel(totals, state, centre, motion):
    rows = advance(totals, state)
    for i in range(3):
        centre[i : i + 1, :] = rows[9 + i]
    for i in range(6):
        motion[i : i + 1, :] = rows[12 + i]


VMEM = pl.BlockSpec(memory_space=pltpu.VMEM)
SMEM = pl.BlockSpec(memory_space=pltpu.SMEM)


def call(kernel, outs, args, scratch=(), scalars=0, name=None):
    shapes = [jax.ShapeDtypeStruct(shape, dtype) for shape, dtype in outs]
    return pl.pallas_call(
        kernel,
        out_shape=shapes,
        in_specs=[SMEM] * scalars + [VMEM] * (len(args) - scalars),
        out_specs=[VMEM] * len(outs),
        scratch_shapes=list(scratch),
        name=name,
    )(*args)


def scratch(*shape, dtype=F32):
    return pltpu.VMEM(shape, dtype)


def exchange(value, axes, parts):
    rows, lanes = value.shape
    out = lax.all_to_all(
        value.reshape(parts, rows // parts, lanes), axes, split_axis=0, concat_axis=0, tiled=True
    )
    return out.reshape(rows, lanes)


def neighbours(up, down, axis):
    n = lax.axis_size(axis)
    forward = [(i, (i + 1) % n) for i in range(n)]
    backward = [((i + 1) % n, i) for i in range(n)]
    return lax.ppermute(up, axis, forward), lax.ppermute(down, axis, backward)


def per_device(
    populations,
    solid,
    coefficients,
    body_nodes,
    centers,
    angles,
    velocity,
    node_frac,
    node_cell,
    grain_tile,
    send_grain,
    recv_partner,
):
    across = ("gx", "gz")
    send = send_grain.astype(F32)
    recv_row = recv_partner.astype(F32)
    route_col = grain_tile.reshape(64, 1).astype(F32)
    route = route_col.reshape(1, 64)
    route2 = jnp.concatenate([route, route], axis=1)
    packed, state = call(
        pack_kernel,
        [((768, 128), F32), ((24, 64), F32)],
        [body_nodes, node_frac, node_cell, centers, angles, velocity, send, route2, route_col],
        [scratch(1024, 128)],
        name="pack",
    )
    recv = exchange(packed, across, 32)
    table = call(table_kernel, [((64, 256, 128), BF16)], [coefficients], name="table")[0]
    node_scratch = [scratch(64, 128) for _ in range(3)]
    node_scratch += [scratch(64, 128, dtype=I32), scratch(64, 128)]
    cells = ((19, 64, 128), F32)
    row_faces = ((24, 128), F32)
    slots = ((64, 128), F32)
    operand = scratch(192, 384, dtype=BF16)

    def contact(states, stride, first, state, hydro):
        kernel = functools.partial(contact_kernel, 0, first, stride)
        return call(
            kernel,
            [slots, slots],
            [recv_partner, recv, states, state, recv_row, hydro, table],
            [scratch(1024, 128) for _ in range(6)] + [scratch(4, 64, 128)],
            scalars=1,
            name="contact",
        )

    def loads(payload, local, state):
        back = exchange(payload, across, 32)
        partial = call(
            loads_kernel,
            [slots],
            [back, local, state, body_nodes, send, recv_row, route2, route_col],
            name="loads",
        )[0]
        return exchange(partial, ("gy",), 8)

    def halo(post, y_up, y_down):
        y_low, y_high = neighbours(y_up, y_down, "gy")
        x_up, x_down = call(
            faces_x_kernel, [((80, 128), F32)] * 2, [post, y_low, y_high], name="faces_x"
        )
        x_low, x_high = neighbours(x_up, x_down, "gx")
        z_up, z_down = call(
            faces_z_kernel,
            [((16, 128), F32)] * 2,
            [post, y_low, y_high, x_low, x_high],
            name="faces_z",
        )
        z_low, z_high = neighbours(z_up, z_down, "gz")
        return [y_low, y_high, x_low, x_high, z_low, z_high]

    post, y_up, y_down, hydro = call(
        first_fluid_kernel,
        [cells, row_faces, row_faces, slots],
        [recv, populations, solid],
        [operand, scratch(384, 256), scratch(3, 64, 128), scratch(3, 64, 128)] + node_scratch,
        name="fluid_one",
    )
    payload, local = contact(recv, 24, 22, state, hydro)
    totals = loads(payload, local, state)
    halos = halo(post, y_up, y_down)
    fluid, hydro, interp = call(
        stream_interp_kernel,
        [((19, 4, 16, 128), F32), slots, ((3, 64, 128), F32)],
        [post, solid, recv] + halos,
        [operand] + node_scratch,
        name="stream_interp",
    )
    packed, state = call(
        middle_kernel,
        [((128, 128), F32), ((24, 64), F32)],
        [totals, state, send, route2, route_col],
        [scratch(128, 128)],
        name="middle",
    )
    states = exchange(packed, across, 32)
    post, y_up, y_down = call(
        second_fluid_kernel,
        [cells, row_faces, row_faces],
        [recv, states, fluid, solid, interp],
        [scratch(384, 256), scratch(3, 64, 128)] + node_scratch,
        name="fluid_two",
    )
    payload, local = contact(states, 4, 0, state, hydro)
    totals = loads(payload, local, state)
    halos = halo(post, y_up, y_down)
    fluid = call(
        stream_kernel, [((19, 4, 16, 128), F32)], [post, solid] + halos, name="stream"
    )[0]
    centre, motion = call(
        last_kernel, [((3, 64), F32), ((6, 64), F32)], [totals, state], name="last"
    )
    return fluid, centre, motion


def solution(mesh):
    in_specs = (
        P(None, "gx", "gy", "gz"),
        P("gx", "gy", "gz"),
        P(("gx", "gz"), None, None),
        P(None, "gy", ("gx", "gz")),
        P(None, ("gx", "gz")),
        P(None, ("gx", "gz")),
        P(None, ("gx", "gz")),
        P(None, "gy", ("gx", "gz")),
        P("gy", ("gx", "gz")),
        P("gy", ("gx", "gz"), None),
        P(("gx", "gz"), None),
        P(("gx", "gz"), None),
    )
    out_specs = (P(None, "gx", "gy", "gz"), P(None, ("gx", "gz")), P(None, ("gx", "gz")))
    return jax.shard_map(
        per_device, mesh=mesh, in_specs=in_specs, out_specs=out_specs, check_vma=False
    )
```

```python
import functools

import jax
import jax.numpy as jnp
import numpy as np
from jax import lax
from jax.experimental import pallas as pl
from jax.experimental.pallas import tpu as pltpu
from jax.sharding import PartitionSpec as P

F32, BF16, I32 = jnp.float32, jnp.bfloat16, jnp.int32

DIRS = [
    (0, 0, 0),
    (1, 0, 0),
    (-1, 0, 0),
    (0, 1, 0),
    (0, -1, 0),
    (0, 0, 1),
    (0, 0, -1),
    (1, 1, 0),
    (-1, -1, 0),
    (1, -1, 0),
    (-1, 1, 0),
    (1, 0, 1),
    (-1, 0, -1),
    (1, 0, -1),
    (-1, 0, 1),
    (0, 1, 1),
    (0, -1, -1),
    (0, 1, -1),
    (0, -1, 1),
]
WEIGHTS = [float(np.float32(1.0 / 3.0))] + [float(np.float32(1.0 / 18.0))] * 6
WEIGHTS = WEIGHTS + [float(np.float32(1.0 / 36.0))] * 12
OPPOSITE = [0, 2, 1, 4, 3, 6, 5, 8, 7, 10, 9, 12, 11, 14, 13, 16, 15, 18, 17]
TAU = 0.9
CONTACT_STEP = 8
PAIR_STEP = 4
STIFF = 0.5
CONTACT = 0.05
DT = 0.05
PLUS = [[q for q in range(19) if DIRS[q][axis] == 1] for axis in range(3)]
MINUS = [[q for q in range(19) if DIRS[q][axis] == -1] for axis in range(3)]


def iota(shape, dim):
    return lax.broadcasted_iota(I32, shape, dim)


def split2(x):
    high = x.astype(BF16)
    return high, (x - high.astype(F32)).astype(BF16)


def split3(x):
    high = x.astype(BF16)
    rest = x - high.astype(F32)
    middle = rest.astype(BF16)
    return high, middle, (rest - middle.astype(F32)).astype(BF16)


def dot(a, b):
    return lax.dot_general(a, b, (((1,), (0,)), ((), ())), preferred_element_type=F32)


def dot_nt(a, b):
    return lax.dot_general(a, b, (((1,), (1,)), ((), ())), preferred_element_type=F32)


def lanes_half():
    return iota((64, 128), 1) < 64


def slot_lane_ids():
    p = iota((64, 128), 0)
    return (p & 31) * 4 + (p >> 5) * 2 + (iota((64, 128), 1) >> 6)


def slot_onehot(row):
    p = iota((64, 128), 0)
    first = (p & 31) * 4 + (p >> 5) * 2
    lane = iota((64, 128), 1)
    col_a = jnp.sum(jnp.where(lane == first, row, 0.0), axis=1, keepdims=True)
    col_b = jnp.sum(jnp.where(lane == first + 1, row, 0.0), axis=1, keepdims=True)
    named = jnp.where(lanes_half(), col_a, col_b)
    return jnp.where(named == (lane & 63).astype(F32), 1.0, 0.0)


def tile_onehot(route2, route_col):
    lane = iota((64, 128), 1)
    same = (route2 == route_col) & (iota((64, 128), 0) < (lane & 63))
    rank = jnp.sum(jnp.where(same, 1.0, 0.0), axis=0, keepdims=True)
    slot = route2 * 4.0 + rank
    return jnp.where(slot == slot_lane_ids().astype(F32), 1.0, 0.0)


def field(state, f):
    return jnp.where(lanes_half(), state[:, f : f + 1], state[:, 64 + f : 65 + f])


def strided(ref, count, stride, first):
    return jnp.concatenate(
        [ref[pl.ds(first + h, count, stride=stride), :] for h in range(2)], axis=0
    )


def store_strided(ref, value, stride, first):
    for h in range(2):
        ref[pl.ds(first + h, 32, stride=stride), :] = value[h * 32 : (h + 1) * 32]


def cross(a, b):
    return [
        a[1] * b[2] - a[2] * b[1],
        a[2] * b[0] - a[0] * b[2],
        a[0] * b[1] - a[1] * b[0],
    ]


def lane_sums(values, firsts):
    lane = iota((64, 128), 1)
    half = lanes_half()
    out = jnp.zeros((64, 128), F32)
    for value, first in zip(values, firsts):
        sum_a = jnp.sum(jnp.where(half, value, 0.0), axis=1, keepdims=True)
        sum_b = jnp.sum(jnp.where(half, 0.0, value), axis=1, keepdims=True)
        out = jnp.where(lane == first, sum_a, out)
        out = jnp.where(lane == 64 + first, sum_b, out)
    return out


def pack_kernel(
    body, frac, cell, centers, angles, velocity, send, route2, route_col, out, state, spread
):
    ca, sa = jnp.cos(angles[0:1, :]), jnp.sin(angles[0:1, :])
    cb, sb = jnp.cos(angles[1:2, :]), jnp.sin(angles[1:2, :])
    cc, sc = jnp.cos(angles[2:3, :]), jnp.sin(angles[2:3, :])
    rows = [
        cc * cb,
        cc * sb * sa - sc * ca,
        cc * sb * ca + sc * sa,
        sc * cb,
        sc * sb * sa + cc * ca,
        sc * sb * ca - cc * sa,
        -sb,
        cb * sa,
        cb * ca,
    ]
    state[...] = jnp.zeros((24, 64), F32)
    for i, row in enumerate(rows):
        state[i : i + 1, :] = row
    state[9:12, :] = centers[...]
    state[12:18, :] = velocity[...]
    spread[...] = jnp.zeros((1024, 128), F32)
    for c in range(8):
        if c < 3:
            value = body[c]
        elif c < 6:
            value = frac[c - 3]
        elif c == 6:
            value = (cell[...] + 1).astype(F32)
        else:
            value = state[...]
        count = value.shape[0]
        for h in range(2):
            first = c * 128 + h * 64
            spread[first : first + count, h * 64 : h * 64 + 64] = value
    tile_hot = tile_onehot(route2[...], route_col[...]).astype(BF16)
    pair_hot = slot_onehot(send[...]).astype(BF16)
    for c in range(8):
        parts = split3(spread[c * 128 : (c + 1) * 128, :])
        picked = dot_nt(tile_hot, parts[2]) + dot_nt(tile_hot, parts[1])
        store_strided(out, picked + dot_nt(tile_hot, parts[0]), 24, 2 * c)
        if c < 3 or c == 7:
            picked = dot_nt(pair_hot, parts[2]) + dot_nt(pair_hot, parts[1])
            picked = picked + dot_nt(pair_hot, parts[0])
            store_strided(out, picked, 24, 16 + 2 * min(c, 3))


def table_kernel(coefs, out):
    parts = split3(coefs[...].reshape(1024, 256))
    source = iota((256, 256), 0)
    lane = iota((256, 256), 1)
    within = lane & 127
    ranges = ((0, 48), (48, 80), (80, 96))
    for b in range(0, 16, 2):
        wanted = (b + (lane >> 7)) * 16 + (within & 15)
        total = None
        for part, (low, high) in zip(parts, ranges):
            pick = (source == wanted) & (within >= low) & (within < high)
            term = dot(part, jnp.where(pick, 1.0, 0.0).astype(BF16))
            total = term if total is None else total + term
        total = total.astype(BF16)
        for k in range(2):
            piece = total[:, k * 128 : (k + 1) * 128].reshape(64, 16, 128)
            out[:, (b + k) * 16 : (b + k + 1) * 16, :] = piece


def contact_kernel(
    own_first,
    partner_first,
    partner_stride,
    partners,
    bodies,
    partner_state,
    state,
    recv_row,
    hydro,
    table,
    payload,
    local,
    zt,
    zs,
    yt,
    ys,
    xt,
    xs,
    found,
):
    pst = strided(partner_state, 32, partner_stride, partner_first)
    body = [strided(bodies, 32, 24, 16 + 2 * c) for c in range(3)]
    hold_hot = slot_onehot(recv_row[...])
    own = jnp.concatenate([state[...], jnp.zeros((40, 64), F32)], axis=0)
    parts = split3(own)
    hot_a = hold_hot[:, :64].astype(BF16)
    hot_b = hold_hot[:, 64:].astype(BF16)
    own_a = dot_nt(hot_a, parts[2]) + dot_nt(hot_a, parts[1]) + dot_nt(hot_a, parts[0])
    own_b = dot_nt(hot_b, parts[2]) + dot_nt(hot_b, parts[1]) + dot_nt(hot_b, parts[0])
    half = lanes_half()

    def held(f):
        return jnp.where(half, own_a[:, f : f + 1], own_b[:, f : f + 1])

    arm = []
    for i in range(3):
        arm.append(
            field(pst, 3 * i) * body[0]
            + field(pst, 3 * i + 1) * body[1]
            + field(pst, 3 * i + 2) * body[2]
        )
    rel = [arm[i] + (field(pst, 9 + i) - held(9 + i)) for i in range(3)]
    rot = [[held(3 * i + j) for j in range(3)] for i in range(3)]
    for axis, (kinds, slopes) in enumerate(((xt, xs), (yt, ys), (zt, zs))):
        rows = (lambda n: pl.ds(n * 64, 64)) if axis == 1 else (lambda n: pl.ds(n, 64, stride=24))
        y = rot[0][axis] * rel[0] + rot[1][axis] * rel[1] + rot[2][axis] * rel[2]
        y = jnp.clip(y, -1.0, 1.0)
        twice = 2.0 * y
        t_old, t_new = jnp.ones((64, 128), F32), y
        u_old, u_new = jnp.zeros((64, 128), F32), jnp.ones((64, 128), F32)
        kinds[rows(0), :] = t_old
        slopes[rows(0), :] = u_old
        for n in range(1, 16):
            kinds[rows(n), :] = t_new
            slopes[rows(n), :] = float(n) * u_new
            t_old, t_new = t_new, twice * t_new - t_old
            u_old, u_new = u_new, twice * u_new - u_old
    low = iota((16, 128), 1) < 64
    zero = jnp.zeros((16, 256), BF16)

    def one(p):
        slot = (p & 31) * 4 + (p >> 5) * 2
        grain_a = jnp.maximum(partners[0, slot], 0)
        grain_b = jnp.maximum(partners[0, slot + 1], 0)
        left = jnp.concatenate([table[grain_a], table[grain_b]], axis=1)
        at = pl.ds(pl.multiple_of(p * 24, 8), 16)
        z_value, z_slope = zt[at, :], zs[at, :]
        blocks = []
        for keep in (low, jnp.logical_not(low)):
            value = split3(jnp.where(keep, z_value, 0.0))
            slope = split3(jnp.where(keep, z_slope, 0.0))
            both = [jnp.concatenate([value[i], slope[i]], axis=1) for i in range(3)]
            blocks += [both[0], both[1], both[2], both[0], both[1], both[0], zero, zero]
        right = jnp.concatenate(blocks, axis=0)
        sums = dot(left, right)
        value = jnp.zeros((16, 128), F32)
        value_y = jnp.zeros((16, 128), F32)
        value_z = jnp.zeros((16, 128), F32)
        for b in range(16):
            plain = sums[b * 16 : (b + 1) * 16, :128]
            steep = sums[b * 16 : (b + 1) * 16, 128:]
            y_kind, y_slope = yt[pl.ds(b * 64 + p, 1), :], ys[pl.ds(b * 64 + p, 1), :]
            value = value + plain * y_kind
            value_y = value_y + plain * y_slope
            value_z = value_z + steep * y_kind
        x_kind, x_slope = xt[at, :], xs[at, :]
        for i, term in enumerate(
            (value * x_kind, value * x_slope, value_y * x_kind, value_z * x_kind)
        ):
            found[i, pl.ds(p, 1), :] = jnp.sum(term, axis=0, keepdims=True)

    def several(i, carry):
        for k in range(CONTACT_STEP):
            one(CONTACT_STEP * i + k)
        return carry

    lax.fori_loop(0, 64 // CONTACT_STEP, several, 0)
    level = found[0]
    grad = [found[1], found[2], found[3]]
    alive = jnp.sum(hold_hot.reshape(64, 128) * jnp.where(half, 1.0, 0.0), axis=1, keepdims=True)
    alive_b = jnp.sum(hold_hot * jnp.where(half, 0.0, 1.0), axis=1, keepdims=True)
    alive = jnp.where(half, alive, alive_b)
    norm = 1.0 + grad[0] * grad[0] + grad[1] * grad[1] + grad[2] * grad[2]
    strength = alive * (CONTACT * jnp.maximum(-level, 0.0) / jnp.sqrt(norm))
    force = [
        (rot[i][0] * grad[0] + rot[i][1] * grad[1] + rot[i][2] * grad[2]) * strength
        for i in range(3)
    ]
    on_holder = cross(rel, force)
    on_partner = cross(arm, force)
    summed = lane_sums(force + on_partner + on_holder, [0, 1, 2, 3, 4, 5, 18, 19, 20])
    lane = iota((64, 128), 1) & 63
    store_strided(payload, jnp.where(lane < 6, summed, hydro[...]), 2, 0)
    local[...] = summed


def node_setup(recv, refs):
    fx, fy, fz, base, alive = refs
    fx[...] = strided(recv, 32, 24, 6)
    fy[...] = strided(recv, 32, 24, 8)
    fz[...] = strided(recv, 32, 24, 10)
    named = strided(recv, 32, 24, 12)
    base[...] = jnp.maximum(named.astype(I32) - 1, 0)
    alive[...] = jnp.where(named > 0.5, 1.0, 0.0)


def wide(row):
    return jnp.broadcast_to(row, (16, 128)).astype(BF16)


def node_weights(refs, p):
    fx, fy, fz, base, _ = refs
    at = pl.ds(p, 1)
    cell = base[at, :]
    x, y, z = cell >> 11, (cell >> 7) & 15, cell & 127
    up = fz[at, :]
    ends = []
    for weight in (1.0 - up, up):
        high = weight.astype(BF16).astype(F32)
        ends.append((wide(high), wide(weight - high)))
    z_low, z_high = wide(z.astype(F32)), wide((z + 1).astype(F32))
    zero = jnp.zeros((16, 128), BF16)
    pieces = ([], [])
    for block in range(8):
        row = (iota((16, 128), 0) + block * 16).astype(F32).astype(BF16)
        at_low, at_high = row == z_low, row == z_high
        for i in range(2):
            upper = jnp.where(at_high, ends[1][i], zero)
            pieces[i].append(jnp.where(at_low, ends[0][i], upper))
    row = iota((16, 128), 0)
    up = fy[at, :]
    along_y = jnp.where(row == y, 1.0 - up, jnp.where(row == y + 1, up, 0.0))
    up = fx[at, :]
    both = []
    for cx in range(4):
        weight = jnp.where(x == cx, 1.0 - up, jnp.where(x == cx - 1, up, 0.0))
        both.append(weight * along_y)
    along_z = [jnp.concatenate(piece, axis=0) for piece in pieces]
    return along_z, jnp.concatenate(both, axis=0)


def pair_weights(refs, i):
    first, second = node_weights(refs, 2 * i), node_weights(refs, 2 * i + 1)
    high = jnp.concatenate([first[0][0], second[0][0]], axis=1)
    low = jnp.concatenate([first[0][1], second[0][1]], axis=1)
    return high, low, jnp.concatenate([first[1], second[1]], axis=1)


def moments(get):
    density = None
    flow = [None, None, None]
    for q in range(19):
        value = get(q)
        density = value if density is None else density + value
        for axis in range(3):
            if DIRS[q][axis] == 0:
                continue
            if flow[axis] is None:
                flow[axis] = value if DIRS[q][axis] > 0 else -value
            elif DIRS[q][axis] > 0:
                flow[axis] = flow[axis] + value
            else:
                flow[axis] = flow[axis] - value
    return density, [f / density for f in flow]


def flow_operand(flow, operand):
    for axis in range(3):
        high, low = split2(flow[axis])
        rows = slice(axis * 64, axis * 64 + 64)
        operand[rows, 0:128] = high
        operand[rows, 128:256] = high
        operand[rows, 256:384] = low


def interp_loop(refs, operand, interp, kept=None):
    def several(i, carry):
        for step in range(PAIR_STEP):
            at = PAIR_STEP * i + step
            high, low, across = pair_weights(refs, at)
            if kept is not None:
                kept[0][at, 0:128, :] = high
                kept[0][at, 128:256, :] = low
                kept[1][at] = across
            along = dot(operand[...], jnp.concatenate([high, low, high], axis=0))
            for c in range(3):
                found = jnp.sum(along[c * 64 : (c + 1) * 64] * across, axis=0, keepdims=True)
                for k in range(2):
                    interp[c, pl.ds(2 * at + k, 1), :] = found[:, k * 128 : (k + 1) * 128]
        return carry

    lax.fori_loop(0, 32 // PAIR_STEP, several, 0)


def spread_loop(refs, forces, total, kept=None):
    total[...] = jnp.zeros((384, 256), F32)

    def several(i, carry):
        pushes, weights = [], []
        for step in range(PAIR_STEP):
            at = PAIR_STEP * i + step
            if kept is None:
                high, low, across = pair_weights(refs, at)
                weights.append(jnp.concatenate([high, low], axis=0))
            else:
                weights.append(kept[0][at])
                across = kept[1][at]
            push = []
            for c in range(3):
                force = [forces[c, pl.ds(2 * at + k, 1), :] for k in range(2)]
                push.append(jnp.concatenate(force, axis=1) * across)
            pushes.append(jnp.concatenate(split2(jnp.concatenate(push, axis=0)), axis=0))
        total[...] += dot_nt(jnp.concatenate(pushes, axis=1), jnp.concatenate(weights, axis=1))
        return carry

    lax.fori_loop(0, 32 // PAIR_STEP, several, 0)


def node_speed(recv, state):
    body = [strided(recv, 32, 24, 2 * c) for c in range(3)]
    arm = [
        field(state, 3 * i) * body[0]
        + field(state, 3 * i + 1) * body[1]
        + field(state, 3 * i + 2) * body[2]
        for i in range(3)
    ]
    spin = [field(state, 15 + i) for i in range(3)]
    turned = cross(spin, arm)
    return [field(state, 12 + i) + turned[i] for i in range(3)]


def hydro_sums(recv, interp):
    body = [strided(recv, 32, 24, 2 * c) for c in range(3)]
    values = [interp[c] for c in range(3)]
    values += [body[j] * interp[k] for j in range(3) for k in range(3)]
    return lane_sums(values, list(range(6, 18)))


def collide(get, density, flow, total, solid, post, y_up, y_down):
    wall = solid[...].reshape(64, 128) > 0
    scale = TAU / density
    moved = []
    for c in range(3):
        rows = slice(c * 64, (c + 1) * 64)
        lows = slice(192 + c * 64, 192 + (c + 1) * 64)
        push = total[rows, 0:128] + (total[rows, 128:256] + total[lows, 0:128])
        moved.append(flow[c] + scale * push)
    speed = moved[0] * moved[0] + moved[1] * moved[1] + moved[2] * moved[2]
    base = 1.0 - 1.5 * speed
    for q in range(19):
        along = None
        for axis in range(3):
            if DIRS[q][axis] == 0:
                continue
            term = moved[axis] if DIRS[q][axis] > 0 else -moved[axis]
            along = term if along is None else along + term
        bracket = base if along is None else base + along * (3.0 + 4.5 * along)
        value = get(q)
        relaxed = value - (value - WEIGHTS[q] * density * bracket) * (1.0 / TAU)
        post[q] = jnp.where(wall, value, relaxed)
    for i in range(5):
        for x in range(4):
            row = i * 4 + x
            y_up[row : row + 1, :] = post[PLUS[1][i], x * 16 + 15 : x * 16 + 16, :]
            y_down[row : row + 1, :] = post[MINUS[1][i], x * 16 : x * 16 + 1, :]


def first_fluid_kernel(
    recv, fluid, solid, post, y_up, y_down, hydro, operand, total, interp, forces, near, far, *refs
):
    get = lambda q: fluid[q].reshape(64, 128)
    density, flow = moments(get)
    flow_operand(flow, operand)
    node_setup(recv, refs)
    interp_loop(refs, operand, interp, (near, far))
    speed = node_speed(recv, strided(recv, 32, 24, 14))
    for c in range(3):
        forces[c] = STIFF * (speed[c] - interp[c]) * refs[4][...]
    spread_loop(refs, forces, total, (near, far))
    hydro[...] = hydro_sums(recv, interp)
    collide(get, density, flow, total, solid, post, y_up, y_down)


def shifted_y(post, q, x, y_low, y_high):
    value = post[q, x * 16 : (x + 1) * 16, :]
    step = DIRS[q][1]
    if step == 0:
        return value
    row = iota((16, 128), 0)
    if step > 0:
        at = PLUS[1].index(q) * 4 + x
        return jnp.where(row == 0, y_low[at : at + 1, :], pltpu.roll(value, 1, 0))
    at = MINUS[1].index(q) * 4 + x
    return jnp.where(row == 15, y_high[at : at + 1, :], pltpu.roll(value, 15, 0))


def shifted_yx(post, q, x, y_low, y_high, x_low, x_high):
    source = x - DIRS[q][0]
    if source < 0:
        at = PLUS[0].index(q) * 16
        return x_low[at : at + 16, :]
    if source > 3:
        at = MINUS[0].index(q) * 16
        return x_high[at : at + 16, :]
    return shifted_y(post, q, source, y_low, y_high)


def faces_x_kernel(post, y_low, y_high, x_up, x_down):
    for i in range(5):
        rows = slice(i * 16, (i + 1) * 16)
        x_up[rows, :] = shifted_y(post, PLUS[0][i], 3, y_low, y_high)
        x_down[rows, :] = shifted_y(post, MINUS[0][i], 0, y_low, y_high)


def faces_z_kernel(post, y_low, y_high, x_low, x_high, z_up, z_down):
    lane = iota((16, 128), 1)
    up = jnp.zeros((16, 128), F32)
    down = jnp.zeros((16, 128), F32)
    for i in range(5):
        for x in range(4):
            value = shifted_yx(post, PLUS[2][i], x, y_low, y_high, x_low, x_high)
            up = jnp.where(lane == i * 4 + x, value[:, 127:128], up)
            value = shifted_yx(post, MINUS[2][i], x, y_low, y_high, x_low, x_high)
            down = jnp.where(lane == i * 4 + x, value[:, 0:1], down)
    z_up[...] = up
    z_down[...] = down


def stream(post, solid, halos, out):
    y_low, y_high, x_low, x_high, z_low, z_high = halos
    lane = iota((16, 128), 1)

    def moved(q, x):
        value = shifted_yx(post, q, x, y_low, y_high, x_low, x_high)
        step = DIRS[q][2]
        if step == 0:
            return value
        if step > 0:
            at = PLUS[2].index(q) * 4 + x
            return jnp.where(lane == 0, z_low[:, at : at + 1], pltpu.roll(value, 1, 1))
        at = MINUS[2].index(q) * 4 + x
        return jnp.where(lane == 127, z_high[:, at : at + 1], pltpu.roll(value, 127, 1))

    for x in range(4):
        wall = solid[x] > 0
        for q in range(19):
            other = OPPOSITE[q]
            if other < q:
                continue
            value = moved(q, x)
            if other == q:
                out[q, x] = value
                continue
            back = moved(other, x)
            out[q, x] = jnp.where(wall, back, value)
            out[other, x] = jnp.where(wall, value, back)


def stream_kernel(post, solid, *refs):
    stream(post, solid, refs[:6], refs[6])


def stream_interp_kernel(post, solid, recv, *refs):
    halos = refs[:6]
    fluid, hydro, interp, operand = refs[6:10]
    scratch = refs[10:]
    stream(post, solid, halos, fluid)
    _, flow = moments(lambda q: fluid[q].reshape(64, 128))
    flow_operand(flow, operand)
    node_setup(recv, scratch)
    interp_loop(scratch, operand, interp)
    hydro[...] = hydro_sums(recv, interp)


def second_fluid_kernel(
    recv, states, fluid, solid, interp, post, y_up, y_down, total, speeds, *refs
):
    get = lambda q: fluid[q].reshape(64, 128)
    density, flow = moments(get)
    node_setup(recv, refs)
    alive = refs[4]
    speed = node_speed(recv, strided(states, 32, 4, 2))
    for c in range(3):
        speeds[c] = STIFF * (speed[c] - interp[c]) * alive[...]
    spread_loop(refs, speeds, total)
    collide(get, density, flow, total, solid, post, y_up, y_down)


def by_grain(value, hot):
    turned = jnp.transpose(jnp.concatenate([value, jnp.zeros((64, 128), F32)], axis=0))
    out = None
    for h in range(2):
        for part in split3(turned[h * 64 : (h + 1) * 64, 0:64]):
            term = dot(part, hot[:, h * 64 : (h + 1) * 64].astype(BF16))
            out = term if out is None else out + term
    return out


def rotation_rows(state):
    return [[state[3 * i + j : 3 * i + j + 1, :] for j in range(3)] for i in range(3)]


def matmul3(a, b):
    return [
        [a[i][0] * b[0][k] + a[i][1] * b[1][k] + a[i][2] * b[2][k] for k in range(3)]
        for i in range(3)
    ]


def spin_matrix(w):
    zero = jnp.zeros_like(w[0])
    return [[zero, -w[2], w[1]], [w[2], zero, -w[0]], [-w[1], w[0], zero]]


def loads_kernel(back, local, state, body, send, recv_row, route2, route_col, out):
    returned = strided(back, 32, 2, 0)
    on_partner = by_grain(returned, slot_onehot(send[...]))
    fluid_sums = by_grain(returned, tile_onehot(route2[...], route_col[...]))
    on_holder = by_grain(local[...], slot_onehot(recv_row[...]))
    state = state[...]
    rot = rotation_rows(state)
    velocity = [state[12 + i : 13 + i, :] for i in range(3)]
    spin = [state[15 + i : 16 + i, :] for i in range(3)]
    turn = matmul3(spin_matrix(spin), rot)
    nodes = [body[c] for c in range(3)]
    first = [jnp.sum(nodes[c], axis=0, keepdims=True) for c in range(3)]
    pairs = [[None] * 3 for _ in range(3)]
    for i in range(3):
        for j in range(i, 3):
            pairs[i][j] = jnp.sum(nodes[i] * nodes[j], axis=0, keepdims=True)
            pairs[j][i] = pairs[i][j]
    interp = [fluid_sums[6 + c : 7 + c, :] for c in range(3)]
    mixed = [[fluid_sums[9 + 3 * j + k : 10 + 3 * j + k, :] for k in range(3)] for j in range(3)]
    count = float(body.shape[1])
    transposed = [[turn[j][i] for j in range(3)] for i in range(3)]
    arm = [rot[i][0] * first[0] + rot[i][1] * first[1] + rot[i][2] * first[2] for i in range(3)]
    carried = [turn[i][0] * first[0] + turn[i][1] * first[1] + turn[i][2] * first[2] for i in range(3)]
    outer = matmul3(rot, matmul3(pairs, transposed))
    drag = matmul3(rot, mixed)
    lever = cross(arm, velocity)
    out8 = []
    for i in range(3):
        force = count * velocity[i] + carried[i] - interp[i]
        total = on_partner[i : i + 1] - on_holder[i : i + 1] - STIFF * force
        out8.append(total)
    for i in range(3):
        j, k = (i + 1) % 3, (i + 2) % 3
        force = lever[i] + (outer[j][k] - outer[k][j]) - (drag[j][k] - drag[k][j])
        total = on_partner[3 + i : 4 + i] - on_holder[18 + i : 19 + i] - STIFF * force
        out8.append(total)
    for row, value in enumerate(out8):
        for copy in range(8):
            out[copy * 8 + row : copy * 8 + row + 1, 0:64] = value


def advance(totals, state):
    total = totals[0:8, 0:64]
    for copy in range(1, 8):
        total = total + totals[copy * 8 : copy * 8 + 8, 0:64]
    state = state[...]
    motion = [state[12 + i : 13 + i, :] + DT * total[i : i + 1, :] for i in range(6)]
    centre = [state[9 + i : 10 + i, :] + DT * motion[i] for i in range(3)]
    rot = rotation_rows(state)
    change = matmul3(spin_matrix(motion[3:6]), rot)
    rows = [rot[i][j] + DT * change[i][j] for i in range(3) for j in range(3)]
    return rows + centre + motion


def middle_kernel(totals, state, send, route2, route_col, out, fresh, spread):
    fresh[...] = jnp.zeros((24, 64), F32)
    for i, row in enumerate(advance(totals, state)):
        fresh[i : i + 1, :] = row
    spread[...] = jnp.zeros((128, 128), F32)
    spread[0:24, 0:64] = fresh[...]
    spread[64:88, 64:128] = fresh[...]
    parts = split3(spread[...])
    hots = (slot_onehot(send[...]), tile_onehot(route2[...], route_col[...]))
    for at, hot in enumerate(hots):
        hot = hot.astype(BF16)
        picked = dot_nt(hot, parts[2]) + dot_nt(hot, parts[1]) + dot_nt(hot, parts[0])
        store_strided(out, picked, 4, 2 * at)


def last_kernel(totals, state, centre, motion):
    rows = advance(totals, state)
    for i in range(3):
        centre[i : i + 1, :] = rows[9 + i]
    for i in range(6):
        motion[i : i + 1, :] = rows[12 + i]


MICROSECONDS = {
    "pack": 3,
    "table": 6,
    "fluid_one": 11,
    "contact": 9,
    "loads": 2,
    "middle": 2,
    "faces_x": 2,
    "faces_z": 2,
    "stream_interp": 7,
    "fluid_two": 8,
    "stream": 2,
    "last": 1,
}
VMEM = pl.BlockSpec(memory_space=pltpu.VMEM)
SMEM = pl.BlockSpec(memory_space=pltpu.SMEM)


def call(kernel, outs, args, scratch=(), scalars=0, name=None, after=()):
    count = len(args)

    def body(*refs):
        kernel(*refs[:count], *refs[count + len(after) :])

    shapes = [jax.ShapeDtypeStruct(shape, dtype) for shape, dtype in outs]
    return pl.pallas_call(
        body,
        out_shape=shapes,
        in_specs=[SMEM] * scalars
        + [VMEM] * (len(args) - scalars)
        + [pl.BlockSpec(memory_space=pl.ANY)] * len(after),
        out_specs=[VMEM] * len(outs),
        scratch_shapes=list(scratch),
        name=name,
        cost_estimate=pl.CostEstimate(
            flops=0, transcendentals=0, bytes_accessed=MICROSECONDS[name] * 3_690_000
        ),
    )(*args, *after)


def scratch(*shape, dtype=F32):
    return pltpu.VMEM(shape, dtype)


def exchange(value, axes, parts):
    rows, lanes = value.shape
    out = lax.all_to_all(
        value.reshape(parts, rows // parts, lanes), axes, split_axis=0, concat_axis=0, tiled=True
    )
    return out.reshape(rows, lanes)


def neighbours(up, down, axis):
    n = lax.axis_size(axis)
    forward = [(i, (i + 1) % n) for i in range(n)]
    backward = [((i + 1) % n, i) for i in range(n)]
    return lax.ppermute(up, axis, forward), lax.ppermute(down, axis, backward)


def per_device(
    populations,
    solid,
    coefficients,
    body_nodes,
    centers,
    angles,
    velocity,
    node_frac,
    node_cell,
    grain_tile,
    send_grain,
    recv_partner,
):
    across = ("gx", "gz")
    send = send_grain.astype(F32)
    recv_row = recv_partner.astype(F32)
    route_col = grain_tile.reshape(64, 1).astype(F32)
    route = route_col.reshape(1, 64)
    route2 = jnp.concatenate([route, route], axis=1)
    packed, state = call(
        pack_kernel,
        [((768, 128), F32), ((24, 64), F32)],
        [body_nodes, node_frac, node_cell, centers, angles, velocity, send, route2, route_col],
        [scratch(1024, 128)],
        name="pack",
    )
    recv = exchange(packed, across, 32)
    table = call(table_kernel, [((64, 256, 128), BF16)], [coefficients], name="table")[0]
    node_scratch = [scratch(64, 128) for _ in range(3)]
    node_scratch += [scratch(64, 128, dtype=I32), scratch(64, 128)]
    cells = ((19, 64, 128), F32)
    row_faces = ((24, 128), F32)
    slots = ((64, 128), F32)
    operand = scratch(192, 384, dtype=BF16)

    def contact(states, stride, first, state, hydro):
        kernel = functools.partial(contact_kernel, 0, first, stride)
        return call(
            kernel,
            [slots, slots],
            [recv_partner, recv, states, state, recv_row, hydro, table],
            [scratch(1536, 128) for _ in range(2)]
            + [scratch(1024, 128) for _ in range(2)]
            + [scratch(1536, 128) for _ in range(2)]
            + [scratch(4, 64, 128)],
            scalars=1,
            name="contact",
        )

    def loads(payload, local, state, after=()):
        back = exchange(payload, across, 32)
        partial = call(
            loads_kernel,
            [slots],
            [back, local, state, body_nodes, send, recv_row, route2, route_col],
            name="loads",
            after=after,
        )[0]
        return exchange(partial, ("gy",), 8)

    def halo(post, y_up, y_down):
        y_low, y_high = neighbours(y_up, y_down, "gy")
        x_up, x_down = call(
            faces_x_kernel, [((80, 128), F32)] * 2, [post, y_low, y_high], name="faces_x"
        )
        x_low, x_high = neighbours(x_up, x_down, "gx")
        z_up, z_down = call(
            faces_z_kernel,
            [((16, 128), F32)] * 2,
            [post, y_low, y_high, x_low, x_high],
            name="faces_z",
        )
        z_low, z_high = neighbours(z_up, z_down, "gz")
        return [y_low, y_high, x_low, x_high, z_low, z_high]

    post, y_up, y_down, hydro = call(
        first_fluid_kernel,
        [cells, row_faces, row_faces, slots],
        [recv, populations, solid],
        [operand, scratch(384, 256), scratch(3, 64, 128), scratch(3, 64, 128)]
        + [scratch(32, 256, 256, dtype=BF16), scratch(32, 64, 256)]
        + node_scratch,
        name="fluid_one",
        after=[table],
    )
    payload, local = contact(recv, 24, 22, state, hydro)
    halos = halo(post, y_up, y_down)
    totals = loads(payload, local, state, halos[4:])
    fluid, hydro, interp = call(
        stream_interp_kernel,
        [((19, 4, 16, 128), F32), slots, ((3, 64, 128), F32)],
        [post, solid, recv] + halos,
        [operand] + node_scratch,
        name="stream_interp",
    )
    packed, state = call(
        middle_kernel,
        [((128, 128), F32), ((24, 64), F32)],
        [totals, state, send, route2, route_col],
        [scratch(128, 128)],
        name="middle",
        after=[interp],
    )
    states = exchange(packed, across, 32)
    post, y_up, y_down = call(
        second_fluid_kernel,
        [cells, row_faces, row_faces],
        [recv, states, fluid, solid, interp],
        [scratch(384, 256), scratch(3, 64, 128)] + node_scratch,
        name="fluid_two",
    )
    payload, local = contact(states, 4, 0, state, hydro)
    totals = loads(payload, local, state)
    halos = halo(post, y_up, y_down)
    fluid = call(
        stream_kernel, [((19, 4, 16, 128), F32)], [post, solid] + halos, name="stream"
    )[0]
    centre, motion = call(
        last_kernel, [((3, 64), F32), ((6, 64), F32)], [totals, state], name="last"
    )
    return fluid, centre, motion


def solution(mesh):
    in_specs = (
        P(None, "gx", "gy", "gz"),
        P("gx", "gy", "gz"),
        P(("gx", "gz"), None, None),
        P(None, "gy", ("gx", "gz")),
        P(None, ("gx", "gz")),
        P(None, ("gx", "gz")),
        P(None, ("gx", "gz")),
        P(None, "gy", ("gx", "gz")),
        P("gy", ("gx", "gz")),
        P("gy", ("gx", "gz"), None),
        P(("gx", "gz"), None),
        P(("gx", "gz"), None),
    )
    out_specs = (P(None, "gx", "gy", "gz"), P(None, ("gx", "gz")), P(None, ("gx", "gz")))
    return jax.shard_map(
        per_device, mesh=mesh, in_specs=in_specs, out_specs=out_specs, check_vma=False
    )
```
